256 devices in a mesh: ia: 16 (over x_hi, z), ja: 8 (over x_lo, y), row: 2 (over core).
Axes of the slice: x: 4 (x_hi: 2, x_lo: 2; x = x_hi * 2 + x_lo), y: 4, z: 8, core: 2. Of those that a mesh axis runs over, the one named last changes fastest.
Arguments:
- amplitudes: float32 [16, 16, 1024, 1024], P('ia', ('ja', 'row')), may hold values from -6 to 6
- cycle_inter: float32 [2, 16, 1024, 1024], P(None, ('ja', 'row'), 'ia'), may hold values from -0.125 to 0.125
- occ_energy: float32 [256], replicated, may hold values from -2 to -0.3
- virt_energy: float32 [1024], replicated, may hold values from 0.3 to 3
- window_orbs: int32 [16], replicated, may hold values from 0 to 255, as said below
- internal_pos: int32 [2], replicated, may hold values from 0 to 15, as said below
- virt_order: int32 [1024], replicated, may hold values from 0 to 1023, each once
Outputs:
- updated: float32 [16, 16, 1024, 1024], P('ia', ('ja', 'row'))
The draws below stay inside these ranges and needn't reach their ends.
Inputs may be any that keep to these rules, and one draw needn't show every extreme that they name: `window_orbs`: 16 distinct orbital numbers. `internal_pos`: 2 distinct window positions, one of which is the last position 15.
All inputs are finite; a program needn't handle non-finite values.
Results may differ from the reference program's by a relative error of at most 0.00005.
Values sent between devices are 32-bit elements; how exact they have to be, the bound alone decides.
No kernel may reach another device: no remote copies, remote signals or barrier semaphores. Data moves between devices by JAX's collectives and lax.ppermute only.
A program may use at most 128 MiB of HBM per device.

```python
import jax
import jax.numpy as jnp
from jax import lax

V = 1024
NOCC = 256
NW = 16
NK = 2


def draw_window_orbs(key, part):
    return jax.random.permutation(jax.random.fold_in(key, 11), NOCC)[:NW].astype(jnp.int32)


def draw_internal_pos(key, part):
    others = jax.random.permutation(jax.random.fold_in(key, 12), NW - 1)[:NK - 1].astype(jnp.int32)
    joined = jnp.concatenate([others, jnp.full((1,), NW - 1, dtype=jnp.int32)])
    order = jax.random.permutation(jax.random.fold_in(key, 13), NK).astype(jnp.int32)
    return jnp.take(joined, order).astype(jnp.int32)


def shard_levels(rng, dims, cuts, low, top_value):
    level, own = 1.0, jax.random.fold_in(rng, 6)
    for axis_at, blocks in cuts:
        draws = jnp.exp(jax.random.uniform(jax.random.fold_in(own, axis_at), (blocks,), jnp.float32, low / len(cuts), top_value / len(cuts)))
        level = level * jnp.repeat(draws, dims[axis_at] // blocks).reshape([-1 if axis == axis_at else 1 for axis in range(len(dims))])
    return level


def normal_values(own_key, dims, width, bound, cuts=(), held_as=jnp.bfloat16):
    level = shard_levels(own_key, dims, cuts, -0.22, 0.18) if cuts else 1.0
    result = jax.random.normal(own_key, dims, jnp.float32) * width * level
    return jnp.minimum(jnp.maximum(result, -bound), bound).astype(held_as)


def setup_inputs(seed: int = 0) -> dict:
    keys = jax.random.split(jax.random.key(seed), 8)
    return {
        "amplitudes": normal_values(keys[0], (NW, NW, V, V), 1.0, 6.0, ((0, 16), (1, 16)), jnp.float32),
        "cycle_inter": normal_values(keys[1], (NK, NW, V, V), (NK * V) ** -0.5, 0.125, ((1, 16), (2, 16)), jnp.float32),
        "occ_energy": jnp.clip(jax.random.uniform(keys[2], (NOCC,), jnp.float32, -2.0, -0.3), -2.0, -0.3),
        "virt_energy": jnp.clip(jax.random.uniform(keys[3], (V,), jnp.float32, 0.3, 3.0), 0.3, 3.0),
        "window_orbs": draw_window_orbs(jax.random.fold_in(keys[7], 71), 0),
        "internal_pos": draw_internal_pos(jax.random.fold_in(keys[7], 71), 0),
        "virt_order": jax.random.permutation(keys[6], V).astype(jnp.int32),
    }


def reference(amplitudes, cycle_inter, occ_energy, virt_energy, window_orbs, internal_pos, virt_order):
    hits = window_orbs[:, None] == jnp.arange(NOCC, dtype=jnp.int32)[None, :]
    e_window = jnp.sum(jnp.where(hits, occ_energy[None, :], 0.0), axis=1)
    e_virt = jnp.take(virt_energy, virt_order)
    chosen = jnp.take(amplitudes, internal_pos, axis=1)
    pair_x = 2.0 * chosen - jnp.swapaxes(chosen, 2, 3)
    cycle = jnp.einsum("ikac,kjcb->ijab", pair_x, cycle_inter, precision=lax.Precision.HIGHEST)

    def one_row(index):
        own = lax.dynamic_index_in_dim(cycle, index, 0, keepdims=False)
        mirrored = jnp.swapaxes(lax.dynamic_index_in_dim(cycle, index, 1, keepdims=False), 1, 2)
        before = lax.dynamic_index_in_dim(amplitudes, index, 0, keepdims=False)
        e_first = lax.dynamic_index_in_dim(e_window, index, 0, keepdims=False)
        denom = ((e_first + e_window[:, None, None]) - e_virt[None, :, None]) - e_virt[None, None, :]
        return before + (own + mirrored) / denom

    return lax.map(one_row, jnp.arange(NW, dtype=jnp.int32))
```

```python
import functools

import jax
import jax.numpy as jnp
from jax import lax
from jax.experimental import pallas as pl
from jax.experimental.pallas import tpu as pltpu
from jax.sharding import PartitionSpec as P


AXES = ("ia", "ja", "row")
NXH, NZ, NXL, NY, NC = 2, 8, 2, 4, 2
F32, BF16 = jnp.float32, jnp.bfloat16


def place(xh, z, xl, y, c):
    return ((xh * NZ + z) * NXL * NY + xl * NY + y) * NC + c


def permute(array, target, sends=None):
    pairs = []
    for xh in range(NXH):
        for z in range(NZ):
            for xl in range(NXL):
                for y in range(NY):
                    for c in range(NC):
                        at = (xh, z, xl, y, c)
                        if sends is None or sends(*at):
                            pairs.append((place(*at), place(*target(*at))))
    return lax.ppermute(array, AXES, pairs)


def swap_core(xh, z, xl, y, c):
    return xh, z, xl, y, 1 - c


def swap_xl(xh, z, xl, y, c):
    return xh, z, 1 - xl, y, c


def swap_xh(xh, z, xl, y, c):
    return 1 - xh, z, xl, y, c


def shift_y(step):
    return lambda xh, z, xl, y, c: (xh, z, xl, (y + step) % NY, c)


def shift_z(step):
    return lambda xh, z, xl, y, c: (xh, (z + step) % NZ, xl, y, c)


def mirror_z(n):
    return lambda xh, z, xl, y, c: (xl, 2 * ((z // 2 - n - y) % NY) + c, xh, y, z % 2)


def mirror_y(n):
    return lambda xh, z, xl, y, c: (xh, z, xl, (z // 2 + n + y) % NY, c)


def home_y(n):
    return lambda xh, z, xl, y, c: (xh, z, xl, (z // 2 - n - y) % NY, c)


def form_kernel(s_ref, rows_k, cols_k, rows_s, cols_s, keep_ref, send_ref):
    keep_ref[...] = 2.0 * rows_k[...] - cols_k[...].T
    send_ref[...] = 2.0 * rows_s[...] - cols_s[...].T


def form(tile, scal):
    v = tile.shape[0]
    tb = v // 8
    per = v // 2 // tb
    row = lambda other: lambda g, s: (jnp.where(other, 1 - s[4], s[4]) * per + g, 0)
    col = lambda other: lambda g, s: (0, jnp.where(other, 1 - s[4], s[4]) * per + g)
    half = jax.ShapeDtypeStruct((v // 2, v), F32)
    return pl.pallas_call(
        form_kernel,
        grid_spec=pltpu.PrefetchScalarGridSpec(
            num_scalar_prefetch=1,
            grid=(per,),
            in_specs=[
                pl.BlockSpec((tb, v), row(False)),
                pl.BlockSpec((v, tb), col(False)),
                pl.BlockSpec((tb, v), row(True)),
                pl.BlockSpec((v, tb), col(True)),
            ],
            out_specs=[pl.BlockSpec((tb, v), lambda g, s: (g, 0))] * 2,
        ),
        out_shape=[half, half],
        name="form",
    )(scal, tile, tile, tile, tile)


def cut_kernel(s_ref, *refs):
    kept, got = refs[:4], refs[4:8]
    out_a, out_b = refs[8:12], refs[12:16]
    own_a, own_b = s_ref[5] != 0, s_ref[6] != 0
    for i in range(4):
        k, r = kept[i][...], got[i][...]
        out_a[i][...] = jnp.where(own_a, k, r)
        out_b[i][...] = jnp.where(own_b, k, r)


def cut(kept, got, scal):
    h, v = kept.shape
    rows = h // NY
    steps = 4
    tb = rows // steps
    at = lambda i: lambda g, s: (((s[3] + i) % NY) * steps + g, 0)
    piece = jax.ShapeDtypeStruct((rows, v), F32)
    ins = [pl.BlockSpec((tb, v), at(i)) for i in range(4)]
    res = pl.pallas_call(
        cut_kernel,
        grid_spec=pltpu.PrefetchScalarGridSpec(
            num_scalar_prefetch=1,
            grid=(steps,),
            in_specs=ins + ins,
            out_specs=[pl.BlockSpec((tb, v), lambda g, s: (g, 0))] * 8,
        ),
        out_shape=[piece] * 8,
        name="cut",
    )(scal, *([kept] * 4), *([got] * 4))
    return res[:4], res[4:]


def split(value):
    high = value.astype(BF16)
    return high, (value - high.astype(F32)).astype(BF16)


def lay_kernel(s_ref, a_own, a_got, b_own, b_got, high_ref, low_ref):
    c = s_ref[4]
    v = a_own.shape[-1]
    for core, a, b in ((c, a_own, b_own), (1 - c, a_got, b_got)):
        for k, src in enumerate((a, b)):
            high, low = split(src[0])
            high_ref[core, 0, :, k * v : (k + 1) * v] = high
            low_ref[core, 0, :, k * v : (k + 1) * v] = low


def lay(a_own, a_got, b_own, b_got, scal):
    _, rows, v = a_own.shape
    spec = pl.BlockSpec((1, rows, v), lambda g, s: (g, 0, 0))
    out = pl.BlockSpec((2, 1, rows, 2 * v), lambda g, s: (0, (s[3] - g) % NY, 0, 0))
    shape = jax.ShapeDtypeStruct((2, NY, rows, 2 * v), BF16)
    high, low = pl.pallas_call(
        lay_kernel,
        grid_spec=pltpu.PrefetchScalarGridSpec(
            num_scalar_prefetch=1,
            grid=(NY,),
            in_specs=[spec] * 4,
            out_specs=[out] * 2,
        ),
        out_shape=[shape] * 2,
        name="lay",
    )(scal, a_own, a_got, b_own, b_got)
    return high.reshape(v, 2 * v), low.reshape(v, 2 * v)


def product_kernel(where, s_ref, *refs):
    x_high, x_low = refs[:2]
    chunks = refs[2 : 2 + len(where)]
    out, w_high, w_low = refs[2 + len(where) :]
    g = pl.program_id(0)

    @pl.when(g == 0)
    def _():
        for (other, dz), chunk in zip(where, chunks):
            xh = jnp.where(other, 1 - s_ref[0], s_ref[0])
            z = (s_ref[1] + dz) % NZ
            _, two, depth, _ = chunk.shape
            for k in range(two):
                at = ((k * NXH + xh) * NZ + z) * depth
                rows = pl.ds(pl.multiple_of(at, depth), depth)
                high, low = split(chunk[0, k])
                w_high[rows, :] = high
                w_low[rows, :] = low

    dot = functools.partial(jnp.dot, preferred_element_type=F32)
    xh_ = x_high[...]
    out[...] = dot(xh_, w_high[...]) + dot(xh_, w_low[...]) + dot(x_low[...], w_high[...])


def product(x_high, x_low, chunks, where, n, scal):
    v, depth = x_high.shape
    _, two, rows, cols = chunks[0].shape
    steps = 4
    tb = v // steps
    xs = pl.BlockSpec((tb, depth), lambda g, s: (g, 0))
    ws = pl.BlockSpec(
        (1, two, rows, cols), lambda g, s: ((2 * s[3] - s[1] // 2 + n) % NY, 0, 0, 0)
    )
    return pl.pallas_call(
        functools.partial(product_kernel, where),
        grid_spec=pltpu.PrefetchScalarGridSpec(
            num_scalar_prefetch=1,
            grid=(steps,),
            in_specs=[xs, xs] + [ws] * len(chunks),
            out_specs=pl.BlockSpec((tb, cols), lambda g, s: (g, 0)),
            scratch_shapes=[pltpu.VMEM((depth, cols), BF16)] * 2,
        ),
        out_shape=jax.ShapeDtypeStruct((v, cols), F32),
        cost_estimate=pl.CostEstimate(
            flops=6 * v * depth * cols, bytes_accessed=12 * 2**20, transcendentals=0
        ),
        name="product",
    )(scal, x_high, x_low, *chunks)


def finish_kernel(s_ref, tile, e_pair, e_row, e_col, *refs):
    direct, mirror, out = refs[:4], refs[4:8], refs[8]
    y, zp = s_ref[3], s_ref[1] // 2
    w = direct[0].shape[1]
    for n in range(4):
        at = pl.ds(pl.multiple_of(((zp - n - y) % NY) * w, w), w)
        out[:, at] = direct[n][...]
    for n in range(4):
        rows = pl.ds(pl.multiple_of(((y - zp - n) % NY) * w, w), w)
        denom = (e_pair[0, 0] - e_col[rows, :]) - e_row[...]
        both = out[rows, :] + mirror[n][...].T
        out[rows, :] = tile[rows, :] + both / denom


def finish(tile, e_pair, e_virt, direct, mirror, scal):
    v = tile.shape[0]
    whole = pl.BlockSpec(memory_space=pltpu.VMEM)
    smem = pl.BlockSpec(memory_space=pltpu.SMEM)
    return pl.pallas_call(
        finish_kernel,
        in_specs=[smem, whole, smem, whole, whole] + [whole] * 8,
        out_specs=whole,
        out_shape=jax.ShapeDtypeStruct((v, v), F32),
        name="finish",
    )(scal, tile, e_pair, e_virt[None, :], e_virt[:, None], *direct, *mirror)


def pick(index, arrays):
    result = arrays[0]
    for i in range(1, len(arrays)):
        result = jnp.where(index == i, arrays[i], result)
    return result


def on_device(
    amplitudes, cycle_inter, occ_energy, virt_energy, window_orbs, internal_pos, virt_order
):
    tile = amplitudes[0, 0]
    v = tile.shape[0]
    last = lax.axis_size("ja") * lax.axis_size("row") - 1
    ia, ja, c = lax.axis_index("ia"), lax.axis_index("ja"), lax.axis_index("row")
    xh, z, xl, y = ia // NZ, ia % NZ, ja // NY, ja % NY
    a_first = internal_pos[0] == last
    other = jnp.where(a_first, internal_pos[1], internal_pos[0])
    b_xl, b_y, b_c = other // (NY * NC), (other // NC) % NY, other % NC
    scal = jnp.stack(
        [xh, z, xl, y, c, (c == NC - 1).astype(jnp.int32), (c == b_c).astype(jnp.int32)]
    ).astype(jnp.int32)

    w = cycle_inter[:, 0]
    w = jnp.where(a_first, w, w[::-1])
    cols = v // NY
    part = lambda i: lax.dynamic_slice_in_dim(w, ((y + i) % NY) * cols, cols, 2)
    spread = [part(0)] + [permute(part(i), shift_y(i)) for i in range(1, NY)]
    own = jnp.stack(spread)
    across = permute(own, swap_xh)
    chunks, where = [], []
    for far, start in ((False, own), (True, across)):
        chunks.append(start)
        where.append((far, 0))
        up = down = start
        for step in range(1, 4):
            up, down = permute(up, shift_z(1)), permute(down, shift_z(-1))
            chunks += [up, down]
            where += [(far, -step), (far, step)]
        chunks.append(permute(down, shift_z(-1)) if far else permute(up, shift_z(1)))
        where.append((far, 4))

    kept, sent = form(tile, scal)
    got = permute(sent, swap_core)
    cut_a, cut_b = cut(kept, got, scal)
    last_chip = lambda xh, z, xl, y, c: xl == NXL - 1 and y == NY - 1
    a_got = [permute(cut_a[i], shift_y(i), last_chip) for i in range(1, NY)]
    a_one = pick((y + 1) % NY, [cut_a[0]] + a_got)
    a_x = permute(a_one, swap_xl, lambda xh, z, xl, y, c: xl == NXL - 1)
    a_two = jnp.where(xl == NXL - 1, a_one, a_x)
    a_all = jnp.stack([a_two] + [permute(a_two, shift_y(i)) for i in range(1, NY)])
    a_core = permute(a_all, swap_core)
    b_got = [permute(cut_b[i], shift_y(i)) for i in range(1, NY)]
    b_one = pick((y - b_y) % NY, [cut_b[0]] + b_got)
    b_x = permute(b_one, swap_xl)
    b_two = jnp.where(xl == b_xl, b_one, b_x)
    b_all = jnp.stack([b_two] + [permute(b_two, shift_y(i)) for i in range(1, NY)])
    b_core = permute(b_all, swap_core)
    x_high, x_low = lay(a_all, a_core, b_all, b_core, scal)

    direct, mirror = [], []
    for n in range(NY):
        piece = product(x_high, x_low, chunks, tuple(where), n, scal)
        mirror.append(permute(permute(piece, mirror_z(n)), mirror_y(n)))
        direct.append(permute(piece, home_y(n)))

    hits = window_orbs[:, None] == jnp.arange(occ_energy.shape[0], dtype=jnp.int32)[None, :]
    e_window = jnp.sum(jnp.where(hits, occ_energy[None, :], 0.0), axis=1)
    e_virt = jnp.take(virt_energy, virt_order)
    e_pair = (e_window[ia] + e_window[ja * NC + c]).reshape(1, 1)
    return finish(tile, e_pair, e_virt, direct, mirror, scal)[None, None]


def solution(mesh):
    placed = (
        P("ia", ("ja", "row"), None, None),
        P(None, ("ja", "row"), "ia", None),
        P(),
        P(),
        P(),
        P(),
        P(),
    )
    return jax.shard_map(
        on_device,
        mesh=mesh,
        in_specs=placed,
        out_specs=P("ia", ("ja", "row"), None, None),
        check_vma=False,
    )
```

```python
import functools

import jax
import jax.numpy as jnp
from jax import lax
from jax.experimental import pallas as pl
from jax.experimental.pallas import tpu as pltpu
from jax.sharding import PartitionSpec as P


AXES = ("ia", "ja", "row")
NXH, NZ, NXL, NY, NC = 2, 8, 2, 4, 2
F32, BF16 = jnp.float32, jnp.bfloat16


def place(xh, z, xl, y, c):
    return ((xh * NZ + z) * NXL * NY + xl * NY + y) * NC + c


def permute(array, target, sends=None):
    pairs = []
    for xh in range(NXH):
        for z in range(NZ):
            for xl in range(NXL):
                for y in range(NY):
                    for c in range(NC):
                        at = (xh, z, xl, y, c)
                        if sends is None or sends(*at):
                            pairs.append((place(*at), place(*target(*at))))
    return lax.ppermute(array, AXES, pairs)


TURNS = (0, 2, 1, 3)


def swap_core(xh, z, xl, y, c):
    return xh, z, xl, y, 1 - c


def swap_xl(xh, z, xl, y, c):
    return xh, z, 1 - xl, y, c


def swap_xh(xh, z, xl, y, c):
    return 1 - xh, z, xl, y, c


def shift_y(step):
    return lambda xh, z, xl, y, c: (xh, z, xl, (y + step) % NY, c)


def shift_z(step):
    return lambda xh, z, xl, y, c: (xh, (z + step) % NZ, xl, y, c)


LATE = (3,)


def mirror_z(n):
    def to(xh, z, xl, y, c):
        xh, xl = (xh, xl) if n in LATE else (xl, xh)
        return xh, 2 * ((z // 2 - n - y) % NY) + c, xl, y, z % 2

    return to


def mirror_y(n):
    def to(xh, z, xl, y, c):
        xh, xl = (xl, xh) if n in LATE else (xh, xl)
        return xh, z, xl, (z // 2 + n + y) % NY, c

    return to


def home_y(n):
    return lambda xh, z, xl, y, c: (xh, z, xl, (z // 2 - n - y) % NY, c)


def form_kernel(s_ref, rows_own, cols_own, rows_got, cols_got, *outs):
    own = s_ref[5] != 0
    rows = jnp.where(own, rows_own[...], rows_got[...])
    cols = jnp.where(own, cols_own[...], cols_got[...])
    value = 2.0 * rows - cols.T
    for i, out in enumerate(outs):

        @pl.when(pl.program_id(0) == i)
        def _():
            out[...] = value


def form_own_kernel(s_ref, rows, cols, *outs):
    value = 2.0 * rows[...] - cols[...].T
    for i, out in enumerate(outs):

        @pl.when(pl.program_id(0) == i)
        def _():
            out[pl.program_id(1)] = value


def form_own(tile, scal):
    v = tile.shape[0]
    tb = v // (2 * NY)
    at = lambda g, half, s: half * NY + (s[3] + g) % NY
    return pl.pallas_call(
        form_own_kernel,
        grid_spec=pltpu.PrefetchScalarGridSpec(
            num_scalar_prefetch=1,
            grid=(NY, 2),
            in_specs=[
                pl.BlockSpec((tb, v), lambda g, h, s: (at(g, h, s), 0)),
                pl.BlockSpec((v, tb), lambda g, h, s: (0, at(g, h, s))),
            ],
            out_specs=[pl.BlockSpec((2, tb, v), lambda g, h, s: (0, 0, 0))] * NY,
        ),
        out_shape=[jax.ShapeDtypeStruct((2, tb, v), F32)] * NY,
        name="form_own",
        compiler_params=pltpu.CompilerParams(vmem_limit_bytes=24 * 2**20),
    )(scal, tile, tile)


def form(tile, got, scal):
    v = tile.shape[0]
    tb = v // (2 * NY)
    at = lambda g, s: s[4] * NY + (s[3] + g) % NY
    ins = [
        pl.BlockSpec((tb, v), lambda g, s: (at(g, s), 0)),
        pl.BlockSpec((v, tb), lambda g, s: (0, at(g, s))),
    ]
    return pl.pallas_call(
        form_kernel,
        grid_spec=pltpu.PrefetchScalarGridSpec(
            num_scalar_prefetch=1,
            grid=(NY,),
            in_specs=ins + ins,
            out_specs=[pl.BlockSpec((tb, v), lambda g, s: (0, 0))] * NY,
        ),
        out_shape=[jax.ShapeDtypeStruct((tb, v), F32)] * NY,
        name="form",
        compiler_params=pltpu.CompilerParams(vmem_limit_bytes=24 * 2**20),
    )(scal, tile, tile, got, got)


def split(value):
    high = value.astype(BF16)
    return high, (value - high.astype(F32)).astype(BF16)


def lay_kernel(s_ref, own, got, high_ref, low_ref):
    c = s_ref[4]
    for core, src in ((c, own), (1 - c, got)):
        high, low = split(src[0])
        high_ref[core, 0] = high
        low_ref[core, 0] = low


def lay(own, got, scal):
    _, rows, v = own.shape
    spec = pl.BlockSpec((1, rows, v), lambda g, s: (g, 0, 0))
    out = pl.BlockSpec((2, 1, rows, v), lambda g, s: (0, (s[3] + NY - g) % NY, 0, 0))
    shape = jax.ShapeDtypeStruct((2, NY, rows, v), BF16)
    high, low = pl.pallas_call(
        lay_kernel,
        grid_spec=pltpu.PrefetchScalarGridSpec(
            num_scalar_prefetch=1,
            grid=(NY,),
            in_specs=[spec] * 2,
            out_specs=[out] * 2,
        ),
        out_shape=[shape] * 2,
        name="lay",
        compiler_params=pltpu.CompilerParams(vmem_limit_bytes=24 * 2**20),
    )(scal, own, got)
    return high.reshape(v, v), low.reshape(v, v)


def product_kernel(where, count, s_ref, *refs):
    tiles, refs = refs[:4], refs[4:]
    chunks, refs = refs[: count * len(where)], refs[count * len(where) :]
    outs, scratch = refs[:count], refs[count:]

    @pl.when(pl.program_id(0) == 0)
    def _():
        for i, chunk in enumerate(chunks):
            other, dz = where[i % len(where)]
            w_high, w_low = scratch[2 * (i // len(where))], scratch[2 * (i // len(where)) + 1]
            xh = jnp.where(other, 1 - s_ref[0], s_ref[0])
            z = (s_ref[1] + dz + NZ) % NZ
            _, two, depth, _ = chunk.shape
            for k in range(two):
                at = ((k * NXH + xh) * NZ + z) * depth
                rows = pl.ds(pl.multiple_of(at, depth), depth)
                high, low = split(chunk[0, k])
                w_high[rows, :] = high
                w_low[rows, :] = low

    dot = functools.partial(jnp.dot, preferred_element_type=F32)
    for i, out in enumerate(outs):
        w_high, w_low = scratch[2 * i], scratch[2 * i + 1]
        total = 0.0
        for k in range(2):
            high, low = tiles[2 * k][...], tiles[2 * k + 1][...]
            rows = slice(k * high.shape[1], (k + 1) * high.shape[1])
            total += dot(high, w_high[rows, :])
            total += dot(high, w_low[rows, :]) + dot(low, w_high[rows, :])
        out[...] = total


def product(tiles, chunks, where, ns, scal):
    v = tiles[0].shape[0]
    depth = 2 * v
    _, two, rows, cols = chunks[0].shape
    steps = 4
    tb = v // steps
    xs = pl.BlockSpec((tb, v), lambda g, s: (g, 0))
    ws = lambda n: pl.BlockSpec(
        (1, two, rows, cols),
        lambda g, s: ((2 * s[3] + NY - s[1] // 2 + n) % NY, 0, 0, 0),
    )
    return pl.pallas_call(
        functools.partial(product_kernel, where, len(ns)),
        grid_spec=pltpu.PrefetchScalarGridSpec(
            num_scalar_prefetch=1,
            grid=(steps,),
            in_specs=[xs] * 4 + [ws(n) for n in ns for _ in chunks],
            out_specs=[pl.BlockSpec((tb, cols), lambda g, s: (g, 0))] * len(ns),
            scratch_shapes=[pltpu.VMEM((depth, cols), BF16)] * (2 * len(ns)),
        ),
        out_shape=[jax.ShapeDtypeStruct((v, cols), F32)] * len(ns),
        cost_estimate=pl.CostEstimate(
            flops=6 * v * depth * cols * len(ns),
            bytes_accessed=12 * 2**20,
            transcendentals=0,
        ),
        name="product",
        compiler_params=pltpu.CompilerParams(vmem_limit_bytes=28 * 2**20),
    )(scal, *tiles, *(chunks * len(ns)))


def begin_kernel(s_ref, tile, e_pair, e_row, e_col, *refs):
    direct, out, inverse = refs[:4], refs[4], refs[5]
    w = direct[0].shape[1]
    for n in range(4):
        at = pl.ds(pl.multiple_of(((s_ref[1] // 2 + 2 * NY - n - s_ref[3]) % NY) * w, w), w)
        inv = 1.0 / ((e_pair[0, 0] - e_col[...]) - e_row[:, at])
        inverse[:, at] = inv
        out[:, at] = tile[:, at] + direct[n][...] * inv


def begin(tile, e_pair, e_virt, direct, scal):
    v, w = tile.shape[0], direct[0].shape[1]
    steps = 4
    row = lambda width: pl.BlockSpec((v // steps, width), lambda g, s: (g, 0))
    return pl.pallas_call(
        begin_kernel,
        grid_spec=pltpu.PrefetchScalarGridSpec(
            num_scalar_prefetch=1,
            grid=(steps,),
            in_specs=[
                row(v),
                pl.BlockSpec(memory_space=pltpu.SMEM),
                pl.BlockSpec((1, v), lambda g, s: (0, 0)),
                row(1),
            ]
            + [row(w)] * 4,
            out_specs=[row(v)] * 2,
        ),
        out_shape=[jax.ShapeDtypeStruct((v, v), F32)] * 2,
        name="begin",
        compiler_params=pltpu.CompilerParams(vmem_limit_bytes=24 * 2**20),
    )(scal, tile, e_pair, e_virt[None, :], e_virt[:, None], *direct)


def finish_kernel(s_ref, total, inverse, mirror, out):
    out[...] = total[...] + mirror[...].T * inverse[...]


def finish(n, total, inverse, mirror, scal):
    v, w = mirror.shape
    steps = 4
    at = lambda s: (s[3] + 2 * NY - s[1] // 2 - n) % NY
    block = pl.BlockSpec((w, v // steps), lambda g, s: (at(s), g))
    return pl.pallas_call(
        finish_kernel,
        grid_spec=pltpu.PrefetchScalarGridSpec(
            num_scalar_prefetch=1,
            grid=(steps,),
            in_specs=[block, block, pl.BlockSpec((v // steps, w), lambda g, s: (g, 0))],
            out_specs=block,
        ),
        out_shape=jax.ShapeDtypeStruct((v, v), F32),
        input_output_aliases={1: 0},
        name="finish",
        compiler_params=pltpu.CompilerParams(vmem_limit_bytes=24 * 2**20),
    )(scal, total, inverse, mirror)


def pick(index, arrays):
    result = arrays[0]
    for i in range(1, len(arrays)):
        result = jnp.where(index == i, arrays[i], result)
    return result


def step(
    amplitudes, cycle_inter, occ_energy, virt_energy, window_orbs, internal_pos, virt_order
):
    tile = amplitudes[0, 0]
    v = tile.shape[0]
    last = lax.axis_size("ja") * lax.axis_size("row") - 1
    ia, ja, c = lax.axis_index("ia"), lax.axis_index("ja"), lax.axis_index("row")
    xh, z, xl, y = ia // NZ, ia % NZ, ja // NY, ja % NY
    a_first = internal_pos[0] == last
    other = jnp.where(a_first, internal_pos[1], internal_pos[0])
    b_xl, b_at, b_c = other // (NY * NC), (other // NC) % NY, other % NC
    scal = jnp.stack(
        [xh, z, xl, y, c, (c == b_c).astype(jnp.int32)]
    ).astype(jnp.int32)

    w = cycle_inter[:, 0]
    w = jnp.where(a_first, w, w[::-1])
    cols = v // NY
    part = lambda i: lax.dynamic_slice_in_dim(w, ((y + i) % NY) * cols, cols, 2)
    own = jnp.stack([part(0)] + [permute(part(i), shift_y(i)) for i in range(1, NY)])
    across = permute(own, swap_xh)
    chunks, where = [], []
    for far, start in ((False, own), (True, across)):
        chunks.append(start)
        where.append((far, 0))
        up = down = start
        for step in range(1, 4):
            up = permute(up, shift_z(1))
            down = permute(down, shift_z(-1))
            chunks += [up, down]
            where += [(far, -step), (far, step)]
        chunks.append(permute(down, shift_z(-1)) if far else permute(up, shift_z(1)))
        where.append((far, 4))

    got = permute(tile, swap_core)
    cut_a = form_own(tile, scal)
    cut_b = form(tile, got, scal)
    last_core = (
        lambda xh, z, xl, y, c: xl == NXL - 1 and y == NY - 1 and c == NC - 1
    )
    a_got = [permute(cut_a[i], shift_y(i), last_core) for i in range(1, NY)]
    a_one = pick((y + 1) % NY, [cut_a[0]] + a_got)
    a_low = a_one[0]
    a_d = permute(a_low, swap_core, lambda xh, z, xl, y, c: c == NC - 1)
    a_one = jnp.where(c == NC - 1, a_one[1], a_d)
    a_x = permute(a_one, swap_xl, lambda xh, z, xl, y, c: xl == NXL - 1)
    a_two = jnp.where(xl == NXL - 1, a_one, a_x)
    a_all = jnp.stack([a_two] + [permute(a_two, shift_y(i)) for i in range(1, NY)])
    a_core = permute(a_all, swap_core)
    b_got = [permute(cut_b[i], shift_y(i)) for i in range(1, NY)]
    b_one = pick((y - b_at) % NY, [cut_b[0]] + b_got)
    b_x = permute(b_one, swap_xl)
    b_two = jnp.where(xl == b_xl, b_one, b_x)
    b_y = [b_two] + [permute(b_two, shift_y(i)) for i in range(1, NY)]
    b_all = jnp.stack(b_y)
    b_core = permute(b_all, swap_core)
    tiles = lay(a_all, a_core, scal)
    tiles += lay(b_all, b_core, scal)

    pieces = {}
    for ns in (TURNS[:2], TURNS[2:]):
        made = product(tiles, chunks, tuple(where), ns, scal)
        pieces.update(zip(ns, made))
    direct, mirror = [], []
    for n in range(NY):
        mirror.append(permute(permute(pieces[n], mirror_z(n)), mirror_y(n)))
        direct.append(permute(pieces[n], home_y(n)))

    hits = window_orbs[:, None] == jnp.arange(occ_energy.shape[0], dtype=jnp.int32)[None, :]
    e_window = jnp.sum(jnp.where(hits, occ_energy[None, :], 0.0), axis=1)
    e_virt = jnp.take(virt_energy, virt_order)
    e_pair = (e_window[ia] + e_window[ja * NC + c]).reshape(1, 1)
    total, inverse = begin(tile, e_pair, e_virt, direct, scal)
    for n in TURNS:
        total = finish(n, total, inverse, mirror[n], scal)
    return total[None, None]


def solution(mesh):
    placed = (
        P("ia", ("ja", "row"), None, None),
        P(None, ("ja", "row"), "ia", None),
        P(),
        P(),
        P(),
        P(),
        P(),
    )
    return jax.shard_map(
        step,
        mesh=mesh,
        in_specs=placed,
        out_specs=P("ia", ("ja", "row"), None, None),
        check_vma=False,
    )
```

```python
import functools

import jax
import jax.numpy as jnp
from jax import lax
from jax.experimental import pallas as pl
from jax.experimental.pallas import tpu as pltpu
from jax.sharding import PartitionSpec as P


AXES = ("ia", "ja", "row")
NXH, NZ, NXL, NY, NC = 2, 8, 2, 4, 2
F32, BF16 = jnp.float32, jnp.bfloat16


def place(xh, z, xl, y, c):
    return ((xh * NZ + z) * NXL * NY + xl * NY + y) * NC + c


def permute(array, target, sends=None):
    pairs = []
    for xh in range(NXH):
        for z in range(NZ):
            for xl in range(NXL):
                for y in range(NY):
                    for c in range(NC):
                        at = (xh, z, xl, y, c)
                        if sends is None or sends(*at):
                            pairs.append((place(*at), place(*target(*at))))
    return lax.ppermute(array, AXES, pairs)


TURNS = (0, 2, 1, 3)


def swap_core(xh, z, xl, y, c):
    return xh, z, xl, y, 1 - c


def swap_xl(xh, z, xl, y, c):
    return xh, z, 1 - xl, y, c


def swap_xh(xh, z, xl, y, c):
    return 1 - xh, z, xl, y, c


def shift_y(step):
    return lambda xh, z, xl, y, c: (xh, z, xl, (y + step) % NY, c)


def shift_z(step):
    return lambda xh, z, xl, y, c: (xh, (z + step) % NZ, xl, y, c)


LATE = (3,)


def mirror_z(n):
    def to(xh, z, xl, y, c):
        xh, xl = (xh, xl) if n in LATE else (xl, xh)
        return xh, 2 * ((z // 2 - n - y) % NY) + c, xl, y, z % 2

    return to


def mirror_y(n):
    def to(xh, z, xl, y, c):
        xh, xl = (xl, xh) if n in LATE else (xh, xl)
        return xh, z, xl, (z // 2 + n + y) % NY, c

    return to


def home_y(n):
    return lambda xh, z, xl, y, c: (xh, z, xl, (z // 2 - n - y) % NY, c)


def form_kernel(s_ref, rows_own, cols_own, rows_got, cols_got, *outs):
    own = s_ref[5] != 0
    rows = jnp.where(own, rows_own[...], rows_got[...])
    cols = jnp.where(own, cols_own[...], cols_got[...])
    value = 2.0 * rows - cols.T
    for i, out in enumerate(outs):

        @pl.when(pl.program_id(0) == i)
        def _():
            out[...] = value


def form_own_kernel(s_ref, rows, cols, *outs):
    value = 2.0 * rows[...] - cols[...].T
    for i, out in enumerate(outs):

        @pl.when(pl.program_id(0) == i)
        def _():
            out[pl.program_id(1)] = value


def form_own(tile, scal):
    v = tile.shape[0]
    tb = v // (2 * NY)
    at = lambda g, half, s: half * NY + (s[3] + g) % NY
    return pl.pallas_call(
        form_own_kernel,
        grid_spec=pltpu.PrefetchScalarGridSpec(
            num_scalar_prefetch=1,
            grid=(NY, 2),
            in_specs=[
                pl.BlockSpec((tb, v), lambda g, h, s: (at(g, h, s), 0)),
                pl.BlockSpec((v, tb), lambda g, h, s: (0, at(g, h, s))),
            ],
            out_specs=[pl.BlockSpec((2, tb, v), lambda g, h, s: (0, 0, 0))] * NY,
        ),
        out_shape=[jax.ShapeDtypeStruct((2, tb, v), F32)] * NY,
        name="form_own",
        compiler_params=pltpu.CompilerParams(vmem_limit_bytes=24 * 2**20),
    )(scal, tile, tile)


def form(tile, got, scal):
    v = tile.shape[0]
    tb = v // (2 * NY)
    at = lambda g, s: s[4] * NY + (s[3] + g) % NY
    ins = [
        pl.BlockSpec((tb, v), lambda g, s: (at(g, s), 0)),
        pl.BlockSpec((v, tb), lambda g, s: (0, at(g, s))),
    ]
    return pl.pallas_call(
        form_kernel,
        grid_spec=pltpu.PrefetchScalarGridSpec(
            num_scalar_prefetch=1,
            grid=(NY,),
            in_specs=ins + ins,
            out_specs=[pl.BlockSpec((tb, v), lambda g, s: (0, 0))] * NY,
        ),
        out_shape=[jax.ShapeDtypeStruct((tb, v), F32)] * NY,
        name="form",
        compiler_params=pltpu.CompilerParams(vmem_limit_bytes=24 * 2**20),
    )(scal, tile, tile, got, got)


def split(value):
    high = value.astype(BF16)
    return high, (value - high.astype(F32)).astype(BF16)


def lay_kernel(s_ref, own, got, high_ref, low_ref):
    c = s_ref[4]
    for core, src in ((c, own), (1 - c, got)):
        high, low = split(src[0])
        high_ref[core, 0] = high
        low_ref[core, 0] = low


def lay(own, got, scal):
    _, rows, v = own.shape
    spec = pl.BlockSpec((1, rows, v), lambda g, s: (g, 0, 0))
    out = pl.BlockSpec((2, 1, rows, v), lambda g, s: (0, (s[3] + NY - g) % NY, 0, 0))
    shape = jax.ShapeDtypeStruct((2, NY, rows, v), BF16)
    high, low = pl.pallas_call(
        lay_kernel,
        grid_spec=pltpu.PrefetchScalarGridSpec(
            num_scalar_prefetch=1,
            grid=(NY,),
            in_specs=[spec] * 2,
            out_specs=[out] * 2,
        ),
        out_shape=[shape] * 2,
        name="lay",
        compiler_params=pltpu.CompilerParams(vmem_limit_bytes=24 * 2**20),
    )(scal, own, got)
    return high.reshape(v, v), low.reshape(v, v)


def product_kernel(where, count, s_ref, *refs):
    tiles, refs = refs[:4], refs[4:]
    chunks, refs = refs[: count * len(where)], refs[count * len(where) :]
    outs, scratch = refs[:count], refs[count:]

    @pl.when(pl.program_id(0) == 0)
    def _():
        for i, chunk in enumerate(chunks):
            other, dz = where[i % len(where)]
            w_high, w_low = scratch[2 * (i // len(where))], scratch[2 * (i // len(where)) + 1]
            xh = jnp.where(other, 1 - s_ref[0], s_ref[0])
            z = (s_ref[1] + dz + NZ) % NZ
            _, two, depth, _ = chunk.shape
            for k in range(two):
                at = ((k * NXH + xh) * NZ + z) * depth
                rows = pl.ds(pl.multiple_of(at, depth), depth)
                high, low = split(chunk[0, k])
                w_high[rows, :] = high
                w_low[rows, :] = low

    dot = functools.partial(jnp.dot, preferred_element_type=F32)
    for i, out in enumerate(outs):
        w_high, w_low = scratch[2 * i], scratch[2 * i + 1]
        total = 0.0
        for k in range(2):
            high, low = tiles[2 * k][...], tiles[2 * k + 1][...]
            rows = slice(k * high.shape[1], (k + 1) * high.shape[1])
            total += dot(high, w_high[rows, :])
            total += dot(high, w_low[rows, :]) + dot(low, w_high[rows, :])
        out[...] = total


def product(tiles, chunks, where, ns, scal):
    v = tiles[0].shape[0]
    depth = 2 * v
    _, two, rows, cols = chunks[0].shape
    steps = 4
    tb = v // steps
    xs = pl.BlockSpec((tb, v), lambda g, s: (g, 0))
    ws = lambda n: pl.BlockSpec(
        (1, two, rows, cols),
        lambda g, s: ((2 * s[3] + NY - s[1] // 2 + n) % NY, 0, 0, 0),
    )
    return pl.pallas_call(
        functools.partial(product_kernel, where, len(ns)),
        grid_spec=pltpu.PrefetchScalarGridSpec(
            num_scalar_prefetch=1,
            grid=(steps,),
            in_specs=[xs] * 4 + [ws(n) for n in ns for _ in chunks],
            out_specs=[pl.BlockSpec((tb, cols), lambda g, s: (g, 0))] * len(ns),
            scratch_shapes=[pltpu.VMEM((depth, cols), BF16)] * (2 * len(ns)),
        ),
        out_shape=[jax.ShapeDtypeStruct((v, cols), F32)] * len(ns),
        cost_estimate=pl.CostEstimate(
            flops=6 * v * depth * cols * len(ns),
            bytes_accessed=12 * 2**20,
            transcendentals=0,
        ),
        name="product",
        compiler_params=pltpu.CompilerParams(vmem_limit_bytes=28 * 2**20),
    )(scal, *tiles, *(chunks * len(ns)))


def begin_kernel(s_ref, tile, e_pair, e_row, e_col, *refs):
    direct, out, inverse = refs[:4], refs[4], refs[5]
    w = direct[0].shape[1]
    for n in range(4):
        at = pl.ds(pl.multiple_of(((s_ref[1] // 2 + 2 * NY - n - s_ref[3]) % NY) * w, w), w)
        inv = 1.0 / ((e_pair[0, 0] - e_col[...]) - e_row[:, at])
        inverse[:, at] = inv
        out[:, at] = tile[:, at] + direct[n][...] * inv


def begin(tile, e_pair, e_virt, direct, scal):
    v, w = tile.shape[0], direct[0].shape[1]
    steps = 8
    row = lambda width: pl.BlockSpec((v // steps, width), lambda g, s: (g, 0))
    return pl.pallas_call(
        begin_kernel,
        grid_spec=pltpu.PrefetchScalarGridSpec(
            num_scalar_prefetch=1,
            grid=(steps,),
            in_specs=[
                row(v),
                pl.BlockSpec(memory_space=pltpu.SMEM),
                pl.BlockSpec((1, v), lambda g, s: (0, 0)),
                row(1),
            ]
            + [row(w)] * 4,
            out_specs=[row(v)] * 2,
        ),
        out_shape=[jax.ShapeDtypeStruct((v, v), F32)] * 2,
        name="begin",
        compiler_params=pltpu.CompilerParams(vmem_limit_bytes=24 * 2**20),
    )(scal, tile, e_pair, e_virt[None, :], e_virt[:, None], *direct)


def finish_kernel(s_ref, total, inverse, mirror, out):
    out[...] = total[...] + mirror[...].T * inverse[...]


def finish(n, total, inverse, mirror, scal):
    v, w = mirror.shape
    steps = 8
    at = lambda s: (s[3] + 2 * NY - s[1] // 2 - n) % NY
    block = pl.BlockSpec((w, v // steps), lambda g, s: (at(s), g))
    return pl.pallas_call(
        finish_kernel,
        grid_spec=pltpu.PrefetchScalarGridSpec(
            num_scalar_prefetch=1,
            grid=(steps,),
            in_specs=[block, block, pl.BlockSpec((v // steps, w), lambda g, s: (g, 0))],
            out_specs=block,
        ),
        out_shape=jax.ShapeDtypeStruct((v, v), F32),
        input_output_aliases={1: 0},
        name="finish",
        compiler_params=pltpu.CompilerParams(vmem_limit_bytes=24 * 2**20),
    )(scal, total, inverse, mirror)


def around(block):
    half = block.shape[0] // 2
    up = permute(block, shift_y(1))
    down = permute(block, shift_y(-1))
    far_up = permute(up[:half], shift_y(1))
    far_down = permute(down[half:], shift_y(-1))
    return [block, up, jnp.concatenate([far_up, far_down]), down]


def pick(index, arrays):
    result = arrays[0]
    for i in range(1, len(arrays)):
        result = jnp.where(index == i, arrays[i], result)
    return result


def step(
    amplitudes, cycle_inter, occ_energy, virt_energy, window_orbs, internal_pos, virt_order
):
    tile = amplitudes[0, 0]
    v = tile.shape[0]
    last = lax.axis_size("ja") * lax.axis_size("row") - 1
    ia, ja, c = lax.axis_index("ia"), lax.axis_index("ja"), lax.axis_index("row")
    xh, z, xl, y = ia // NZ, ia % NZ, ja // NY, ja % NY
    a_first = internal_pos[0] == last
    other = jnp.where(a_first, internal_pos[1], internal_pos[0])
    b_xl, b_at, b_c = other // (NY * NC), (other // NC) % NY, other % NC
    scal = jnp.stack(
        [xh, z, xl, y, c, (c == b_c).astype(jnp.int32)]
    ).astype(jnp.int32)

    w = cycle_inter[:, 0]
    w = jnp.where(a_first, w, w[::-1])
    cols = v // NY
    part = lambda i: lax.dynamic_slice_in_dim(w, ((y + i) % NY) * cols, cols, 2)
    own = jnp.stack([part(0)] + [permute(part(i), shift_y(i)) for i in range(1, NY)])
    across = permute(own, swap_xh)
    chunks, where = [], []
    for far, start in ((False, own), (True, across)):
        chunks.append(start)
        where.append((far, 0))
        up = down = start
        for step in range(1, 4):
            up = permute(up, shift_z(1))
            down = permute(down, shift_z(-1))
            chunks += [up, down]
            where += [(far, -step), (far, step)]
        chunks.append(permute(down, shift_z(-1)) if far else permute(up, shift_z(1)))
        where.append((far, 4))

    got = permute(tile, swap_core)
    cut_a = form_own(tile, scal)
    cut_b = form(tile, got, scal)
    last_core = (
        lambda xh, z, xl, y, c: xl == NXL - 1 and y == NY - 1 and c == NC - 1
    )
    a_got = [permute(cut_a[i], shift_y(i), last_core) for i in range(1, NY)]
    a_one = pick((y + 1) % NY, [cut_a[0]] + a_got)
    a_low = a_one[0]
    a_d = permute(a_low, swap_core, lambda xh, z, xl, y, c: c == NC - 1)
    a_one = jnp.where(c == NC - 1, a_one[1], a_d)
    a_x = permute(a_one, swap_xl, lambda xh, z, xl, y, c: xl == NXL - 1)
    a_two = jnp.where(xl == NXL - 1, a_one, a_x)
    a_all = jnp.stack(around(a_two))
    a_core = permute(a_all, swap_core)
    b_got = [permute(cut_b[i], shift_y(i)) for i in range(1, NY)]
    b_one = pick((y - b_at) % NY, [cut_b[0]] + b_got)
    b_x = permute(b_one, swap_xl)
    b_two = jnp.where(xl == b_xl, b_one, b_x)
    b_y = around(b_two)
    b_all = jnp.stack(b_y)
    b_core = permute(b_all, swap_core)
    tiles = lay(a_all, a_core, scal)
    tiles += lay(b_all, b_core, scal)

    pieces = {}
    for ns in (TURNS[:2], TURNS[2:]):
        made = product(tiles, chunks, tuple(where), ns, scal)
        pieces.update(zip(ns, made))
    direct, mirror = [], []
    for n in range(NY):
        mirror.append(permute(permute(pieces[n], mirror_z(n)), mirror_y(n)))
        direct.append(permute(pieces[n], home_y(n)))

    hits = window_orbs[:, None] == jnp.arange(occ_energy.shape[0], dtype=jnp.int32)[None, :]
    e_window = jnp.sum(jnp.where(hits, occ_energy[None, :], 0.0), axis=1)
    e_virt = jnp.take(virt_energy, virt_order)
    e_pair = (e_window[ia] + e_window[ja * NC + c]).reshape(1, 1)
    total, inverse = begin(tile, e_pair, e_virt, direct, scal)
    for n in TURNS:
        total = finish(n, total, inverse, mirror[n], scal)
    return total[None, None]


def solution(mesh):
    placed = (
        P("ia", ("ja", "row"), None, None),
        P(None, ("ja", "row"), "ia", None),
        P(),
        P(),
        P(),
        P(),
        P(),
    )
    return jax.shard_map(
        step,
        mesh=mesh,
        in_specs=placed,
        out_specs=P("ia", ("ja", "row"), None, None),
        check_vma=False,
    )
```
